32 devices in a mesh: blk: 16 (over z, x, core), grp: 2 (over y).
Axes of the slice: x: 2, y: 2, z: 4, core: 2. Of those that a mesh axis runs over, the one named last changes fastest.
Arguments:
- inv_tiles: bfloat16 [32, 32, 512, 512], P(None, 'grp', 'blk'), may hold values from -6 to 6
- factor: bfloat16 [2, 16, 512, 512], P('grp', None, 'blk'), may hold values from -0.0625 to 0.0625
- diag_inv_factor: float32 [2, 512, 512], P('grp', 'blk'), may hold values from -6 to 6
- structure: int32 [2, 16], replicated, may hold values from 0 to 31, as said below
Outputs:
- offdiag_inv: bfloat16 [2, 16, 512, 512], P('grp', None, 'blk')
- diag_inv: float32 [2, 512, 512], P('grp', 'blk')
The draws below stay inside these ranges and needn't reach their ends.
Inputs may be any that keep to these rules, and one draw needn't show every extreme that they name: `structure`: each row lists 16 distinct ancestor blocks in ascending order, exactly 8 in each run of 16 blocks that starts at a multiple of 16; block 31 is listed in every row.
All inputs are finite; a program needn't handle non-finite values.
Results may differ from the reference program's by a relative error of at most 0.018.
Values may be sent and summed in bfloat16 or wider, within the bound.
No kernel may reach another device: no remote copies, remote signals or barrier semaphores. Data moves between devices by JAX's collectives and lax.ppermute only.
A program may use at most 128 MiB of HBM per device.

```python
import jax
import jax.numpy as jnp
from jax import lax

TS = 512
RB = 16
NB = 32
SN = 2
CB = 16
COLSEL = 8


def draw_structure(key, part):
    group_count = RB // COLSEL
    keys = jax.random.split(jax.random.fold_in(key, 17), SN * group_count)

    def choose(subkey):
        shuffled = jax.random.permutation(subkey, CB)
        return jnp.sort(shuffled[:COLSEL])
    picked = jax.vmap(choose)(keys).reshape(SN, group_count, COLSEL).astype(jnp.int32)
    picked = picked.at[:, group_count - 1, COLSEL - 1].set(CB - 1)
    picked = picked.at[0, 0, 0].set(0)
    offsets = jnp.arange(group_count, dtype=jnp.int32)[None, :, None] * CB
    return (picked + offsets).reshape(SN, RB).astype(jnp.int32)


def shard_levels(own_key, extent, pieces, least, largest):
    factor_of = 1.0
    for dim, blocks in pieces:
        heights = jax.random.uniform(jax.random.fold_in(jax.random.fold_in(own_key, 6), dim), (blocks,), jnp.float32, least / len(pieces), largest / len(pieces))
        factor_of = factor_of * jnp.repeat(jnp.exp(heights), extent[dim] // blocks).reshape((-1,) + (1,) * (len(extent) - 1 - dim))
    return factor_of


def gaussian(stream_key, dims, spread, most, shards=(), held_as=jnp.bfloat16):
    result = jax.random.normal(stream_key, dims, jnp.float32) * spread
    if len(shards) > 0:
        result = shard_levels(stream_key, dims, shards, -0.22, 0.18) * result
    return jnp.clip(result, min=-most, max=most).astype(held_as)


def setup_inputs(seed: int = 0) -> dict:
    splits = jax.random.split(jax.random.key(seed), 5)
    return {
        "inv_tiles": gaussian(splits[0], (NB, NB, TS, TS), 1.0, 6.0, ((1, 2), (2, 16))),
        "factor": gaussian(splits[1], (SN, RB, TS, TS), (TS * RB) ** -0.5, 0.0625, ((0, 2), (2, 16))),
        "diag_inv_factor": gaussian(splits[2], (SN, TS, TS), 1.0, 6.0, ((0, 2), (1, 16)), jnp.float32),
        "structure": draw_structure(jax.random.fold_in(splits[4], 71), 0),
    }


def reference(inv_tiles, factor, diag_inv_factor, structure):
    group_count = RB // COLSEL

    def per_node(packed):
        listed, node_factor, node_diag = packed
        gathered = inv_tiles[listed[:, None], listed[None, :]].astype(jnp.float32)
        gathered = gathered.reshape(RB, group_count, COLSEL, TS, TS)
        grouped = node_factor.astype(jnp.float32).reshape(group_count, COLSEL, TS, TS)
        partial_value = jnp.einsum('igjxy,gjyz->gixz', gathered, grouped)
        partial_value = lax.optimization_barrier(partial_value.astype(jnp.bfloat16)).astype(jnp.float32)
        offdiag = (-jnp.sum(partial_value, axis=0)).astype(jnp.bfloat16)
        correction = jnp.einsum('ixy,ixz->yz', node_factor.astype(jnp.float32), offdiag.astype(jnp.float32))
        return offdiag, node_diag - correction

    offdiag_all, diag_all = lax.map(per_node, (structure, factor, diag_inv_factor))
    return offdiag_all, diag_all
```

```python
import functools

import jax
import jax.numpy as jnp
from jax import lax
from jax.experimental import pallas as pl
from jax.experimental.pallas import tpu as pltpu
from jax.sharding import PartitionSpec as P

BF = jnp.bfloat16
F32 = jnp.float32
ANY = pl.BlockSpec(memory_space=pl.ANY)
VM = pl.BlockSpec(memory_space=pltpu.VMEM)


def ring_of_chips(chips):
    outer = 1
    while outer * outer < chips:
        outer *= 2
    if chips % outer:
        outer = chips
    mid = chips // outer
    if mid == 1:
        return outer, mid, list(range(outer))
    walk = []
    for z in range(outer):
        cols = list(range(1, mid))
        for x in cols if z % 2 == 0 else cols[::-1]:
            walk.append(z * mid + x)
    walk += [z * mid for z in range(outer - 1, -1, -1)]
    return outer, mid, walk


def look_up(table, i):
    got = jnp.int32(0)
    for k, v in enumerate(table):
        if v:
            got = got + jnp.where(i == k, jnp.int32(v), jnp.int32(0))
    return got


def run_copies(copies):
    for c in copies:
        c.start()
    for c in copies:
        c.wait()


class Plan:
    def __init__(self, blk, grp, inv, fac):
        self.blk, self.grp = blk, grp
        self.col_local = inv[1]
        self.listed, self.rows, self.width = fac[1], fac[2], fac[3]
        self.per = self.listed // grp
        self.half = self.width // 2
        self.chips = blk // 2
        self.outer, self.mid, self.walk = ring_of_chips(self.chips)
        self.inner = self.mid * 2
        self.pos = [self.walk.index(q) for q in range(self.chips)]
        n = self.chips
        self.swap = [(b, b ^ 1) for b in range(blk)]

        def shift(d):
            return [
                (2 * self.walk[p] + c, 2 * self.walk[(p + d) % n] + c) for p in range(n) for c in (0, 1)
            ]

        self.cw, self.ccw = shift(1), shift(-1)

    def grp_shift(self, d):
        return [(a, (a + d) % self.grp) for a in range(self.grp)]

    def cross_shift(self, d):
        return [
            (b * self.grp + a, (b ^ 1) * self.grp + (a + d) % self.grp)
            for b in range(self.blk)
            for a in range(self.grp)
        ]

    def inner_shift(self, e):
        m = self.inner
        return [(o * m + i, o * m + (i + e) % m) for o in range(self.outer) for i in range(m)]

    def outer_shift(self, f):
        m = self.inner
        return [(o * m + i, (o + f) % self.outer * m + i) for o in range(self.outer) for i in range(m)]


def prepare(plan, fac):
    n = plan.grp - 1

    def body(fac_ref, *refs):
        outs, sem = refs[:-1], refs[-1]
        c = lax.axis_index("blk") % 2
        g = lax.axis_index("grp")
        copies = []
        for d in range(1, plan.grp):
            first = (g + d) % plan.grp * plan.per
            for x in (0, 1):
                cols = (c + x) % 2 * plan.half
                src = fac_ref.at[0, pl.ds(first, plan.per), :, pl.ds(pl.multiple_of(cols, 128), plan.half)]
                k = 2 * (d - 1) + x
                copies.append(pltpu.make_async_copy(src, outs[k], sem.at[k]))
        run_copies(copies)

    shape = jax.ShapeDtypeStruct((plan.per, plan.rows, plan.half), BF)
    return pl.pallas_call(
        body,
        in_specs=[ANY],
        out_specs=[ANY] * (2 * n),
        out_shape=[shape] * (2 * n),
        scratch_shapes=[pltpu.SemaphoreType.DMA((2 * n,))],
        name="prepare",
    )(fac)


def pack_own(plan, fac, fac_other, cuts):
    def body(fac_ref, other_ref, *refs):
        outs, sem = refs[:-1], refs[-1]
        c = lax.axis_index("blk") % 2
        first = lax.axis_index("grp") * plan.per
        cols = pl.ds(pl.multiple_of(c * plan.half, 128), plan.half)
        copies = []
        for k, (lo, hi) in enumerate(cuts):
            for x, ref in enumerate((fac_ref, other_ref)):
                at = pl.multiple_of((c + x) % 2 * plan.rows, plan.rows)
                copies.append(
                    pltpu.make_async_copy(
                        ref.at[0, pl.ds(first + lo, hi - lo), :, cols],
                        outs[k].at[:, pl.ds(at, plan.rows), :],
                        sem.at[2 * k + x],
                    )
                )
        run_copies(copies)

    return pl.pallas_call(
        body,
        in_specs=[ANY] * 2,
        out_specs=[ANY] * len(cuts),
        out_shape=[jax.ShapeDtypeStruct((hi - lo, 2 * plan.rows, plan.half), BF) for lo, hi in cuts],
        scratch_shapes=[pltpu.SemaphoreType.DMA((2 * len(cuts),))],
        name="pack_own",
    )(fac, fac_other)


def pack_others(plan, pieces, cuts):
    spans = []
    for k, (lo, hi) in enumerate(cuts):
        for d in range(plan.grp - 1):
            a, b = max(lo, d * plan.per), min(hi, (d + 1) * plan.per)
            if a < b:
                spans.append((k, d, a - d * plan.per, a - lo, b - a))

    def body(*refs):
        ins, outs, sem = refs[: len(pieces)], refs[len(pieces) : -1], refs[-1]
        c = lax.axis_index("blk") % 2
        copies = []
        for k, d, src, dst, n in spans:
            for x in (0, 1):
                at = pl.multiple_of((c + x) % 2 * plan.rows, plan.rows)
                copies.append(
                    pltpu.make_async_copy(
                        ins[2 * d + x].at[pl.ds(src, n)],
                        outs[k].at[pl.ds(dst, n), pl.ds(at, plan.rows), :],
                        sem.at[len(copies)],
                    )
                )
        run_copies(copies)

    return pl.pallas_call(
        body,
        in_specs=[ANY] * len(pieces),
        out_specs=[ANY] * len(cuts),
        out_shape=[jax.ShapeDtypeStruct((hi - lo, 2 * plan.rows, plan.half), BF) for lo, hi in cuts],
        scratch_shapes=[pltpu.SemaphoreType.DMA((2 * len(spans),))],
        name="pack_others",
    )(*pieces)


def ring(plan, mine, base):
    n, tiles = plan.chips, mine.shape[0]
    shares = [(0, base, mine)]
    cw = ccw = mine
    for k in range(1, (n - 1) // 2 + 1):
        cw = lax.ppermute(cw, "blk", plan.cw)
        ccw = lax.ppermute(ccw, "blk", plan.ccw)
        shares += [(k, base, cw), (n - k, base, ccw)]
    if n % 2 == 0:
        cut = (tiles + 1) // 2
        shares.append((n // 2, base, lax.ppermute(cw[:cut], "blk", plan.cw)))
        if cut < tiles:
            shares.append((n // 2, base + cut, lax.ppermute(ccw[cut:], "blk", plan.ccw)))
    return shares


def start_loads(plan, st_ref, inv_refs, share_refs, shares, nodes, tile_lo, a_ref, b_ref, sem_a, sem_b):
    b = lax.axis_index("blk")
    g = lax.axis_index("grp")
    p = look_up(plan.pos, b // 2)
    lo, n = tile_lo
    for (k, base, _), ref in zip(shares, share_refs):
        q = look_up(plan.walk, (p + plan.chips - k) % plan.chips)
        at = pl.multiple_of(q * (2 * plan.rows), 2 * plan.rows)
        pltpu.make_async_copy(
            ref, b_ref.at[pl.ds(base, ref.shape[0]), pl.ds(at, 2 * plan.rows), :], sem_b
        ).start()
    for t, d in enumerate(nodes):
        s = (g + plan.grp - d) % plan.grp
        for x, inv in enumerate(inv_refs):

            def load(i, _, t=t, s=s, x=x, inv=inv):
                row = st_ref[s, i]
                for j in range(n):
                    col = st_ref[s, g * plan.per + lo + j] - g * plan.col_local
                    pltpu.make_async_copy(
                        inv.at[row, col],
                        a_ref.at[t, x, i, :, pl.ds(j * plan.width, plan.width)],
                        sem_a.at[t, x],
                    ).start()
                return 0

            lax.fori_loop(0, plan.listed, load, 0)


def wait_all(ref, sem):
    pltpu.make_async_copy(ref, ref, sem).wait()


def product(plan, a_ref, b_ref, t, x, n):
    m, k = plan.listed * plan.rows, n * plan.width
    a = a_ref[t, x].reshape(m, k)
    b = b_ref[pl.ds(t * n, n)].reshape(k, plan.half)
    return jnp.dot(a, b, preferred_element_type=F32)


def multiply(plan, st, inv, inv_other, shares, nodes, tile_lo, out_dtype, name):
    lo, n = tile_lo
    m = plan.listed * plan.rows

    def body(st_ref, *refs):
        inv_refs, refs = refs[:2], refs[2:]
        share_refs, (out_ref, a_ref, b_ref, sem_a, sem_b) = refs[: len(shares)], refs[len(shares) :]
        start_loads(plan, st_ref, inv_refs, share_refs, shares, nodes, tile_lo, a_ref, b_ref, sem_a, sem_b)
        wait_all(b_ref, sem_b)
        for t in range(len(nodes)):
            for x in (0, 1):
                wait_all(a_ref.at[t, x], sem_a.at[t, x])
                out_ref[t, x] = product(plan, a_ref, b_ref, t, x, n).astype(out_dtype)

    return pl.pallas_call(
        body,
        in_specs=[pl.BlockSpec(memory_space=pltpu.SMEM)] + [ANY] * (2 + len(shares)),
        out_specs=VM,
        out_shape=jax.ShapeDtypeStruct((len(nodes), 2, m, plan.half), out_dtype),
        scratch_shapes=[
            pltpu.VMEM((len(nodes), 2, plan.listed, plan.rows, n * plan.width), BF),
            pltpu.VMEM((len(nodes) * n, plan.width, plan.half), BF),
            pltpu.SemaphoreType.DMA((len(nodes), 2)),
            pltpu.SemaphoreType.DMA,
        ],
        name=name,
    )(st, inv, inv_other, *[s[2] for s in shares])


def transpose_factor(plan, fac, fac_other):
    m = plan.listed * plan.rows

    def body(a_ref, b_ref, out_ref):
        out_ref[:, pl.ds(0, m)] = a_ref[0].reshape(m, plan.width).T
        out_ref[:, pl.ds(m, m)] = b_ref[0].reshape(m, plan.width).T

    return pl.pallas_call(
        body,
        in_specs=[VM] * 2,
        out_specs=VM,
        out_shape=jax.ShapeDtypeStruct((plan.width, 2 * m), BF),
        name="transpose_factor",
    )(fac, fac_other)


def finish(plan, st, inv, inv_other, shares, tile_lo, before, received, fac_t):
    lo, n = tile_lo
    m = plan.listed * plan.rows
    extra = list(before) + list(received) + [fac_t]
    nb = len(before)

    def body(st_ref, *refs):
        inv_refs, refs = refs[:2], refs[2:]
        share_refs, refs = refs[: len(shares)], refs[len(shares) :]
        extra_refs, refs = refs[: len(extra)], refs[len(extra) :]
        own_ref, other_ref = refs[:2]
        piece_refs, refs = refs[2 : 2 + plan.inner], refs[2 + plan.inner :]
        a_ref, b_ref, o_ref, p_ref = refs[:4]
        extra_bufs, (sem_a, sem_b, sem_e) = refs[4 : 4 + len(extra)], refs[4 + len(extra) :]
        start_loads(plan, st_ref, inv_refs, share_refs, shares, (0,), tile_lo, a_ref, b_ref, sem_a, sem_b)
        loads = [pltpu.make_async_copy(r, v, sem_e.at[k]) for k, (r, v) in enumerate(zip(extra_refs, extra_bufs))]
        for c in loads:
            c.start()
        wait_all(b_ref, sem_b)
        for c in loads[:-1]:
            c.wait()
        for x, out in enumerate((own_ref, other_ref)):
            wait_all(a_ref.at[0, x], sem_a.at[0, x])
            total = product(plan, a_ref, b_ref, 0, x, n)
            for v in extra_bufs[:-1]:
                total = total + v[0, x].astype(F32)
            off = (-total).astype(BF)
            out[...] = off.reshape(plan.listed, plan.rows, plan.half)
            o_ref[pl.ds(x * m, m), :] = off
        loads[-1].wait()
        p_ref[...] = jnp.dot(extra_bufs[-1][...], o_ref[...], preferred_element_type=F32).reshape(p_ref.shape)
        i = lax.axis_index("blk") % plan.inner
        for e, out in enumerate(piece_refs):
            out[...] = p_ref[:, (i + e) % plan.inner].astype(out.dtype)

    slab = jax.ShapeDtypeStruct((plan.listed, plan.rows, plan.half), BF)
    piece = (plan.outer, plan.rows, plan.half)
    return pl.pallas_call(
        body,
        in_specs=[pl.BlockSpec(memory_space=pltpu.SMEM)] + [ANY] * (2 + len(shares) + len(extra)),
        out_specs=[VM] * (2 + plan.inner),
        out_shape=[slab, slab, jax.ShapeDtypeStruct(piece, F32)]
        + [jax.ShapeDtypeStruct(piece, BF)] * (plan.inner - 1),
        scratch_shapes=[
            pltpu.VMEM((1, 2, plan.listed, plan.rows, n * plan.width), BF),
            pltpu.VMEM((n, plan.width, plan.half), BF),
            pltpu.VMEM((2 * m, plan.half), BF),
            pltpu.VMEM((plan.outer, plan.inner, plan.rows, plan.half), F32),
        ]
        + [pltpu.VMEM(v.shape, v.dtype) for v in extra]
        + [
            pltpu.SemaphoreType.DMA((1, 2)),
            pltpu.SemaphoreType.DMA,
            pltpu.SemaphoreType.DMA((len(extra),)),
        ],
        name="finish",
    )(st, inv, inv_other, *[s[2] for s in shares], *extra)


def sum_inner(plan, pieces):
    def body(*refs):
        ins, outs, acc = refs[: plan.inner], refs[plan.inner : -1], refs[-1]
        b = lax.axis_index("blk")
        c, o = b % 2, b // plan.inner
        for x in (0, 1):
            total = ins[x][...].astype(F32)
            for e in range(x + 2, plan.inner, 2):
                total = total + ins[e][...].astype(F32)
            acc[:, :, pl.ds(pl.multiple_of((c + x) % 2 * plan.half, 128), plan.half)] = total
        for f, out in enumerate(outs):
            out[...] = acc[(o + f) % plan.outer].astype(out.dtype)

    shape = (plan.rows, plan.width)
    return pl.pallas_call(
        body,
        in_specs=[VM] * plan.inner,
        out_specs=[VM] * plan.outer,
        out_shape=[jax.ShapeDtypeStruct(shape, F32)] + [jax.ShapeDtypeStruct(shape, BF)] * (plan.outer - 1),
        scratch_shapes=[pltpu.VMEM((plan.outer, plan.rows, plan.width), F32)],
        name="sum_inner",
    )(*pieces)


def sum_outer(plan, dinv, pieces, off_own, off_other):
    def body(d_ref, *refs):
        ins, refs = refs[: plan.outer], refs[plan.outer :]
        own_ref, other_ref, diag_ref, off_ref = refs
        total = ins[0][...]
        for r in ins[1:]:
            total = total + r[...].astype(F32)
        diag_ref[0] = d_ref[0] - total
        c = lax.axis_index("blk") % 2
        for x, r in enumerate((own_ref, other_ref)):
            cols = pl.ds(pl.multiple_of((c + x) % 2 * plan.half, 128), plan.half)
            off_ref[0, :, :, cols] = r[...]

    return pl.pallas_call(
        body,
        in_specs=[VM] * (plan.outer + 3),
        out_specs=[VM] * 2,
        out_shape=[
            jax.ShapeDtypeStruct(dinv.shape, F32),
            jax.ShapeDtypeStruct((1, plan.listed, plan.rows, plan.width), BF),
        ],
        name="sum_outer",
    )(dinv, *pieces, off_own, off_other)


def halves(n):
    cut = (n + 1) // 2
    return [(0, cut), (cut, n)] if cut < n else [(0, n)]


def on_device(plan, inv, fac, dinv, st):
    fac_other = lax.ppermute(fac, "blk", plan.swap)
    sent = prepare(plan, fac)
    received = []
    for d in range(1, plan.grp):
        received.append(lax.ppermute(sent[2 * d - 2], "grp", plan.grp_shift(d)))
        received.append(lax.ppermute(sent[2 * d - 1], ("blk", "grp"), plan.cross_shift(d)))
    own_cuts = halves(plan.per)
    own_mine = pack_own(plan, fac, fac_other, own_cuts)
    inv_other = lax.ppermute(inv, "blk", plan.swap)
    fac_t = transpose_factor(plan, fac, fac_other)
    other_cuts = halves((plan.grp - 1) * plan.per)
    other_mine = pack_others(plan, received, other_cuts)
    others = []
    for (lo, _), mine in zip(other_cuts, other_mine):
        others += ring(plan, mine, lo)
    nodes = tuple(range(1, plan.grp))
    partial = multiply(plan, st, inv, inv_other, others, nodes, (0, plan.per), BF, "multiply_others")
    from_groups = [
        lax.ppermute(partial[d - 1 : d], "grp", plan.grp_shift(plan.grp - d)) for d in range(1, plan.grp)
    ]
    before = []
    for k, (lo, hi) in enumerate(own_cuts):
        shares = ring(plan, own_mine[k], 0)
        if k + 1 < len(own_cuts):
            before.append(multiply(plan, st, inv, inv_other, shares, (0,), (lo, hi - lo), F32, "multiply_own"))
        else:
            out = finish(plan, st, inv, inv_other, shares, (lo, hi - lo), before, from_groups, fac_t)
    off_own, off_partner, pieces = out[0], out[1], out[2:]
    pieces = [pieces[0]] + [
        lax.ppermute(v, "blk", plan.inner_shift(e)) for e, v in enumerate(pieces[1:], 1)
    ]
    off_other = lax.ppermute(off_partner, "blk", plan.swap)
    pieces = sum_inner(plan, pieces)
    pieces = [pieces[0]] + [
        lax.ppermute(v, "blk", plan.outer_shift(f)) for f, v in enumerate(pieces[1:], 1)
    ]
    diag, off = sum_outer(plan, dinv, pieces, off_own, off_other)
    return off, diag


def solution(mesh):
    blk, grp = mesh.shape["blk"], mesh.shape["grp"]

    def call(inv, fac, dinv, st):
        return on_device(Plan(blk, grp, inv.shape, fac.shape), inv, fac, dinv, st)

    return jax.shard_map(
        call,
        mesh=mesh,
        in_specs=(
            P(None, "grp", "blk", None),
            P("grp", None, "blk", None),
            P("grp", "blk", None),
            P(),
        ),
        out_specs=(P("grp", None, "blk", None), P("grp", "blk", None)),
        check_vma=False,
    )
```
